512 devices in a mesh: tmpl: 2 (over x_lo), row: 16 (over y, x_hi, core), col: 16 (over z).
Axes of the slice: x: 4 (x_hi: 2, x_lo: 2; x = x_hi * 2 + x_lo), y: 4, z: 16, core: 2. Of those that a mesh axis runs over, the one named last changes fastest.
Arguments:
- pair: bfloat16 [2, 512, 32768], P('tmpl', 'row', 'col'), may hold values from -6 to 6
- saved_product: bfloat16 [2, 512, 32768], P('tmpl', 'row', 'col'), may hold values from -32 to 32
- out_grad: bfloat16 [2, 512, 32768], P('tmpl', 'row', 'col'), may hold values from -6 to 6
- in_gain: float32 [64], replicated, may hold values from 0.25 to 1.75
- out_gain: float32 [64], replicated, may hold values from 0.25 to 1.75
- w_in: bfloat16 [64, 320], replicated, may hold values from -0.75 to 0.75
- w_out: bfloat16 [64, 64], replicated, may hold values from -0.75 to 0.75
Outputs:
- trunk_grad: float32 [512, 32768], P(('row', 'tmpl'), 'col')
The draws below stay inside these ranges and needn't reach their ends.
All inputs are finite; a program needn't handle non-finite values.
Results may differ from the reference program's by a relative error of at most 0.0067.
Values may be sent and summed in bfloat16 or wider, within the bound.
No kernel may reach another device: no remote copies, remote signals or barrier semaphores. Data moves between devices by JAX's collectives and lax.ppermute only.
A program may use at most 64 MiB of HBM per device.

```python
import jax
import jax.numpy as jnp
from jax import lax

C = 64
TOKENS = 512
TMPL = 2


def block_scale(rng, dims, cuts, low, top_value):
    def one(position, parts):
        steps = jax.random.uniform(jax.random.fold_in(jax.random.fold_in(rng, 6), position), (parts,), jnp.float32, low / len(cuts), top_value / len(cuts))
        return jnp.repeat(jnp.exp(steps), dims[position] // parts).reshape((-1,) + (1,) * (len(dims) - position - 1))

    factor_of = one(*cuts[0])
    for cut in cuts[1:]:
        factor_of = factor_of * one(*cut)
    return factor_of


def scatter_about(own_key, dims, deviation, reach, cuts=(), held_as=jnp.bfloat16):
    array = jax.random.normal(own_key, dims, jnp.float32) * deviation
    if len(cuts) > 0:
        array = block_scale(own_key, dims, cuts, -0.22, 0.18) * array
    return jnp.clip(array, min=-reach, max=reach).astype(held_as)


def setup_inputs(seed: int = 0) -> dict:
    key_list = jax.random.split(jax.random.key(seed), 8)
    pair = scatter_about(key_list[0], (TMPL, TOKENS, TOKENS * C), 1.0, 6.0, ((0, 2), (1, 16), (2, 16)))
    saved_product = scatter_about(key_list[1], (TMPL, TOKENS, TOKENS * C), (0.25 * TOKENS ** 0.5), 32.0, ((0, 2), (1, 16), (2, 16)))
    out_grad = scatter_about(key_list[2], (TMPL, TOKENS, TOKENS * C), 1.0, 6.0, ((0, 2), (1, 16), (2, 16)))
    in_gain = jnp.clip(1.0 + 0.15 * jax.random.normal(key_list[3], (C,), jnp.float32), 0.25, 1.75)
    out_gain = jnp.clip(1.0 + 0.15 * jax.random.normal(key_list[4], (C,), jnp.float32), 0.25, 1.75)
    w_in = scatter_about(key_list[5], (C, 5 * C), C ** -0.5, 0.75)
    w_out = scatter_about(key_list[6], (C, C), C ** -0.5, 0.75)
    return {"pair": pair, "saved_product": saved_product, "out_grad": out_grad, "in_gain": in_gain, "out_gain": out_gain, "w_in": w_in, "w_out": w_out}


EPSILON = 1e-05

def normalize(values, gain):
    centre = values - lax.optimization_barrier(jnp.mean(values, axis=-1, keepdims=True))
    inv_std = lax.rsqrt(lax.optimization_barrier(jnp.mean(centre * centre, axis=-1, keepdims=True)) + EPSILON)
    unit = centre * inv_std
    return (unit * gain, unit, inv_std)

def norm_back(cotangent, unit, inv_std, gain):
    scaled = cotangent * gain
    centred = scaled - lax.optimization_barrier(jnp.mean(scaled, axis=-1, keepdims=True))
    return (centred - unit * lax.optimization_barrier(jnp.mean(scaled * unit, axis=-1, keepdims=True))) * inv_std

def gated_pair(projected, channels):
    left = jax.nn.sigmoid(projected[:, :channels]) * projected[:, channels:2 * channels]
    right = jax.nn.sigmoid(projected[:, 2 * channels:3 * channels]) * projected[:, 3 * channels:4 * channels]
    return (left.astype(jnp.bfloat16), right.astype(jnp.bfloat16))

def gate_grads(projected, d_left, d_right, upstream, mixed_out, out_gate, channels):
    pieces = []
    for offset, d_term in ((0, d_left), (2, d_right)):
        sig_gate = jax.nn.sigmoid(projected[:, offset * channels:(offset + 1) * channels])
        linear = projected[:, (offset + 1) * channels:(offset + 2) * channels]
        pieces.append(d_term * linear * sig_gate * (1.0 - sig_gate))
        pieces.append(d_term * sig_gate)
    pieces.append(upstream * mixed_out * out_gate * (1.0 - out_gate))
    return jnp.concatenate(pieces, axis=-1).astype(jnp.bfloat16)

def one_template(pair, saved, upstream_in, in_gain, out_gain, w_in, w_out):
    channels = in_gain.shape[0]
    normed, in_unit, in_inv = normalize(pair.reshape(-1, channels).astype(jnp.float32), in_gain)
    projected = jnp.dot(normed.astype(jnp.bfloat16), w_in, preferred_element_type=jnp.float32)
    left, right = gated_pair(projected, channels)
    out_norm, out_unit, out_inv = normalize(saved.reshape(-1, channels).astype(jnp.float32), out_gain)
    mixed_out = jnp.dot(out_norm.astype(jnp.bfloat16), w_out, preferred_element_type=jnp.float32)
    upstream = upstream_in.reshape(-1, channels).astype(jnp.float32)
    out_gate = jax.nn.sigmoid(projected[:, 4 * channels:])
    d_mixed = (upstream * out_gate).astype(jnp.bfloat16)
    d_norm = jnp.dot(d_mixed, w_out.T, preferred_element_type=jnp.float32)
    d_product = norm_back(d_norm, out_unit, out_inv, out_gain).astype(jnp.bfloat16)
    shape_three = (TOKENS, TOKENS, channels)
    d_prod_full = d_product.reshape(shape_three).astype(jnp.float32)
    d_left = jnp.einsum('ijc,jkc->ikc', d_prod_full, right.reshape(shape_three).astype(jnp.float32))
    d_right = jnp.einsum('ijc,ikc->jkc', d_prod_full, left.reshape(shape_three).astype(jnp.float32))
    d_proj = gate_grads(projected, d_left.reshape(-1, channels), d_right.reshape(-1, channels), upstream, mixed_out, out_gate, channels)
    d_normed = jnp.dot(d_proj, w_in.T, preferred_element_type=jnp.float32)
    return norm_back(d_normed, in_unit, in_inv, in_gain)

def reference(pair, saved_product, out_grad, in_gain, out_gain, w_in, w_out):
    total = jnp.zeros((TOKENS * TOKENS, in_gain.shape[0]), jnp.float32)
    for template in range(TMPL):
        total = total + one_template(pair[template], saved_product[template], out_grad[template], in_gain, out_gain, w_in, w_out)
    return total.reshape(TOKENS, -1)
```

```python
import jax
import jax.numpy as jnp
from jax import lax
from jax.sharding import PartitionSpec as P

EPSILON = 1e-05
BF16 = jnp.bfloat16
F32 = jnp.float32


def normalize(values, gain):
    centre = values - jnp.mean(values, axis=0, keepdims=True)
    inv_std = lax.rsqrt(jnp.mean(centre * centre, axis=0, keepdims=True) + EPSILON)
    unit = centre * inv_std
    return (unit * gain, unit, inv_std)


def norm_back(cotangent, unit, inv_std, gain):
    scaled = cotangent * gain
    centred = scaled - jnp.mean(scaled, axis=0, keepdims=True)
    return (centred - unit * jnp.mean(scaled * unit, axis=0, keepdims=True)) * inv_std


def channel_major(tile, channels):
    return tile.reshape(-1, channels).T.astype(F32)


def dot(a, b, dims):
    return lax.dot_general(a, b, (dims, ((), ())), preferred_element_type=F32)


def solution(mesh):
    rows_n, cols_n, tmpl_n = mesh.shape["row"], mesh.shape["col"], mesh.shape["tmpl"]

    def body(pair, saved, upstream, in_gain, out_gain, w_in, w_out):
        channels = in_gain.shape[0]
        near = channels // rows_n
        quads = cols_n // near
        pair, saved, upstream = pair[0], saved[0], upstream[0]
        tile_rows, merged = pair.shape
        tile_cols = merged // channels
        half = tile_rows // tmpl_n
        gain_in, gain_out = in_gain[:, None], out_gain[:, None]
        mine = lax.axis_index("tmpl")
        quad = lax.axis_index("col") // near

        both = jnp.concatenate([pair, saved, upstream], axis=0).reshape(3, tmpl_n, half, merged)
        give = lax.dynamic_index_in_dim(both, 1 - mine, 1, keepdims=False)
        keep = lax.dynamic_index_in_dim(both, mine, 1, keepdims=False)
        other = lax.ppermute(give, "tmpl", [(0, 1), (1, 0)])

        def project(pair_cm):
            normed, unit, inv = normalize(pair_cm, gain_in)
            return dot(w_in, normed.astype(BF16), ((0,), (0,))), unit, inv

        proj, _, _ = project(channel_major(pair, channels))
        gate = [proj[n * channels : (n + 1) * channels] for n in range(5)]
        left = (jax.nn.sigmoid(gate[0]) * gate[1]).astype(BF16)
        right = (jax.nn.sigmoid(gate[2]) * gate[3]).astype(BF16)
        _, out_unit, out_inv = normalize(channel_major(saved, channels), gain_out)
        up = channel_major(upstream, channels)
        d_mixed = (up * jax.nn.sigmoid(gate[4])).astype(BF16)
        d_norm = dot(w_out, d_mixed, ((1,), (0,)))
        d_prod = norm_back(d_norm, out_unit, out_inv, gain_out).astype(BF16)

        send = jnp.stack([d_prod, left, right], axis=1).reshape(channels, -1, 128)
        groups = [
            [r * cols_n + near * q + m for r in range(rows_n) for m in range(near)]
            for q in range(quads)
        ]
        got = lax.all_to_all(send, ("row", "col"), 0, 0, axis_index_groups=groups, tiled=True)
        got = got.reshape(rows_n, near, 3, tile_rows, tile_cols).transpose(2, 0, 3, 1, 4)
        got = got.reshape(3, rows_n * tile_rows, near * tile_cols)
        d_own, left_all, right_all = got[0], got[1], got[2]
        width = near * tile_cols
        d_of = [d_own] + [
            lax.ppermute(d_own, "col", [(z, (z - near * s) % cols_n) for z in range(cols_n)])
            for s in range(1, quads)
        ]

        mixed = jnp.concatenate([keep, other], axis=1)
        proj2, in_unit, in_inv = project(channel_major(mixed[0], channels))
        gate2 = [proj2[n * channels : (n + 1) * channels] for n in range(5)]
        normed2, _, _ = normalize(channel_major(mixed[1], channels), gain_out)
        mixed_out = dot(w_out, normed2.astype(BF16), ((0,), (0,)))
        out_gate = jax.nn.sigmoid(gate2[4])
        d_og = (channel_major(mixed[2], channels) * mixed_out * out_gate * (1.0 - out_gate)).astype(BF16)

        right_quads = right_all.reshape(quads, -1, width)
        d_left = jnp.zeros((rows_n * tile_rows, width), F32)
        d_rights = []
        for s in range(quads):
            r_s = lax.dynamic_index_in_dim(right_quads, (quad + s) % quads, 0, keepdims=False)
            d_left = d_left + dot(d_of[s], r_s, ((1,), (0,)))
            d_rights.append(dot(d_of[s], left_all, ((0,), (0,))).astype(BF16))
        twice = jnp.stack(d_rights + d_rights[: quads - 1])
        d_right = lax.dynamic_slice_in_dim(twice, (quads - quad) % quads, quads, 0)
        d_right = d_right.reshape(rows_n * tile_rows, width)
        back = jnp.stack([d_left.astype(BF16), d_right])
        back = back.reshape(2, rows_n, tmpl_n, half, near, tile_cols).transpose(2, 1, 4, 0, 3, 5)
        back = back.reshape(tmpl_n * channels, -1, 128)
        groups = [
            [
                (t * rows_n + r) * cols_n + near * q + m
                for t in range(tmpl_n)
                for r in range(rows_n)
                for m in range(near)
            ]
            for q in range(quads)
        ]
        home = lax.all_to_all(
            back, ("tmpl", "row", "col"), 0, 0, axis_index_groups=groups, tiled=True
        )
        home = home.reshape(tmpl_n, channels, 2, half * tile_cols)
        home = jnp.where(mine == 0, home, home[::-1])
        d_left2, d_right2 = (
            jnp.concatenate([home[0, :, n], home[1, :, n]], axis=1).astype(F32) for n in (0, 1)
        )
        pieces = []
        for d_term, sig, linear in (
            (d_left2, jax.nn.sigmoid(gate2[0]), gate2[1]),
            (d_right2, jax.nn.sigmoid(gate2[2]), gate2[3]),
        ):
            pieces.append((d_term * linear * sig * (1.0 - sig)).astype(BF16))
            pieces.append((d_term * sig).astype(BF16))
        d_proj = jnp.concatenate(pieces + [d_og], axis=0)
        d_normed = dot(w_in, d_proj, ((1,), (0,)))
        grad = norm_back(d_normed, in_unit, in_inv, gain_in)
        cells = half * tile_cols
        grad = grad[:, :cells] + grad[:, cells:]
        return grad.T.reshape(half, merged)

    in_specs = (P("tmpl", "row", "col"),) * 3 + (P(),) * 4
    out_specs = P(("row", "tmpl"), "col")
    return jax.shard_map(body, mesh=mesh, in_specs=in_specs, out_specs=out_specs, check_vma=False)
```

```python
import jax
import jax.numpy as jnp
from jax import lax
from jax.experimental import pallas as pl
from jax.experimental.pallas import tpu as pltpu
from jax.sharding import PartitionSpec as P


EPSILON = 1e-05
BF16 = jnp.bfloat16
F32 = jnp.float32
LANES = 128


def normalize(values, gain):
    scale = 1.0 / values.shape[0]
    centre = values - jnp.sum(values, axis=0, keepdims=True) * scale
    inv_std = lax.rsqrt(jnp.sum(centre * centre, axis=0, keepdims=True) * scale + EPSILON)
    unit = centre * inv_std
    return unit * gain, unit, inv_std


def norm_back(cotangent, unit, inv_std, gain):
    scale = 1.0 / cotangent.shape[0]
    scaled = cotangent * gain
    centred = scaled - jnp.sum(scaled, axis=0, keepdims=True) * scale
    return (centred - unit * (jnp.sum(scaled * unit, axis=0, keepdims=True) * scale)) * inv_std


def dot(a, b, dims):
    return lax.dot_general(a, b, (dims, ((), ())), preferred_element_type=F32)


def column(gain_ref):
    gain = gain_ref[...]
    return jnp.broadcast_to(gain, (LANES, gain.shape[1])).T[:, :1]


def turn(rows):
    turned = jnp.concatenate(rows, axis=0).astype(F32).T
    half = turned.shape[0] // 2
    return jnp.concatenate([turned[:half], turned[half:]], axis=1)


def swap_groups(values, lane):
    count = len(values)
    values = list(values)
    bit = count // 2
    while bit:
        shift = bit * (LANES // count)
        low = (lane & shift) == 0
        for v in range(count):
            if v & bit == 0:
                a, b = values[v], values[v + bit]
                values[v] = jnp.where(low, a, pltpu.roll(b, shift, 1))
                values[v + bit] = jnp.where(low, pltpu.roll(a, LANES - shift, 1), b)
        bit //= 2
    return values


def lanes_of(rows):
    return lax.broadcasted_iota(jnp.int32, (rows, LANES), 1)


def spread_kernel(pair, saved, upstream, in_gain, out_gain, w_in, w_out, send, held):
    channels = w_out.shape[0]
    gain_in, gain_out = column(in_gain), column(out_gain)
    weights, weights_out = w_in[...], w_out[...]
    for b in range(4):

        def tile(ref):
            return turn([ref[0, :, (4 * k + b) * LANES : (4 * k + b + 1) * LANES] for k in range(4)])

        normed, _, _ = normalize(tile(pair), gain_in)
        proj = dot(weights, normed.astype(BF16), ((0,), (0,)))
        gate = [proj[n * channels : (n + 1) * channels] for n in range(5)]
        left = jax.nn.sigmoid(gate[0]) * gate[1]
        right = jax.nn.sigmoid(gate[2]) * gate[3]
        _, unit, inv = normalize(tile(saved), gain_out)
        d_mixed = (tile(upstream) * jax.nn.sigmoid(gate[4])).astype(BF16)
        d_norm = dot(weights_out, d_mixed, ((1,), (0,)))
        d_prod = norm_back(d_norm, unit, inv, gain_out)
        for n, value in enumerate((d_prod, left, right)):
            for p in range(2):
                at = (n * 8 + 2 * b + p) * channels
                held[at : at + channels, :] = value[:, p * LANES : (p + 1) * LANES]
    for c in range(channels):
        send[c] = held[pl.ds(c, 24, stride=channels), :].astype(BF16)


def gather_kernel(got, d_own, left_all, right_all):
    lane = lanes_of(8)
    for n, out in enumerate((d_own, left_all, right_all)):
        for m in range(4):
            for block in range(4):
                parts = swap_groups(
                    [
                        got[(4 * block + r) * 4 + m, n * 8 : (n + 1) * 8, :].astype(F32)
                        for r in range(4)
                    ],
                    lane,
                )
                for k in range(2):
                    out[
                        m * 32 + k * 16 : m * 32 + (k + 1) * 16,
                        block * LANES : (block + 1) * LANES,
                    ] = jnp.concatenate(parts[2 * k : 2 * k + 2], axis=0).astype(BF16)


def product_kernel(quad_ref, left_all, right_all, d0, d1, d2, d3, back, d_left, d_right):
    quad = quad_ref[0]
    total = None
    left = left_all[...]
    for s, d_ref in enumerate((d0, d1, d2, d3)):
        at = pl.multiple_of(lax.rem(quad + s, 4) * LANES, LANES)
        d_s = d_ref[...]
        term = dot(right_all[:, pl.ds(at, LANES)], d_s, ((1,), (0,)))
        total = term if total is None else total + term
        d_right[:, pl.ds(at, LANES)] = dot(left, d_s, ((1,), (1,)))
    d_left[...] = total
    lane = lanes_of(8)
    for m in range(4):
        for block in range(4):
            columns = slice(block * LANES, (block + 1) * LANES)
            chunks = swap_groups(
                [
                    ref[m * 32 + k * 8 : m * 32 + (k + 1) * 8, columns]
                    for ref in (d_left, d_right)
                    for k in range(4)
                ],
                lane,
            )
            for u, chunk in enumerate(chunks):
                r, half = block * 4 + u // 2, u % 2
                back[half * 64 + r * 4 + m] = chunk.astype(BF16)


def prepare_kernel(mine_ref, pair, saved, upstream, other, in_gain, out_gain, w_in, w_out, factors, rest, units, invs):
    channels = w_out.shape[0]
    first = pl.multiple_of(mine_ref[0] * 16, 16)
    gain_in, gain_out = column(in_gain), column(out_gain)
    weights, weights_out = w_in[...], w_out[...]
    for b in range(4):

        def tile(n, ref):
            spans = [slice((4 * k + b) * LANES, (4 * k + b + 1) * LANES) for k in range(4)]
            return turn(
                [ref[0, pl.ds(first, 16), span] for span in spans]
                + [other[n, :, span] for span in spans]
            )

        span = slice(2 * b * LANES, (2 * b + 2) * LANES)
        normed, unit, inv = normalize(tile(0, pair), gain_in)
        units[:, span], invs[:, span] = unit, inv
        proj = dot(weights, normed.astype(BF16), ((0,), (0,)))
        gate = [proj[n * channels : (n + 1) * channels] for n in range(5)]
        for n in range(2):
            sig, linear = jax.nn.sigmoid(gate[2 * n]), gate[2 * n + 1]
            factors[2 * n, :, span] = linear * sig * (1.0 - sig)
            factors[2 * n + 1, :, span] = sig
        normed, _, _ = normalize(tile(1, saved), gain_out)
        mixed = dot(weights_out, normed.astype(BF16), ((0,), (0,)))
        out_gate = jax.nn.sigmoid(gate[4])
        d_og = (tile(2, upstream) * mixed * out_gate * (1.0 - out_gate)).astype(BF16)
        rest[:, span] = dot(weights[:, 4 * channels :], d_og, ((1,), (0,)))


def finish_kernel(mine_ref, home, factors, rest, units, invs, in_gain, w_in, out, held):
    channels = rest.shape[0]
    mine = mine_ref[0]
    gain_in = column(in_gain)
    weights = w_in[:, : 4 * channels]
    for t in range(2):
        base = lax.rem(mine + t, 2) * channels
        for c in range(channels):
            at = (t * channels + c) * 8
            held[at : at + 8, :] = home[base + c].astype(F32)
    low = lanes_of(channels) < LANES // 2
    for b in range(4):
        sums = []
        for p in range(2):
            g = 2 * b + p
            span = slice(g * LANES, (g + 1) * LANES)
            h0 = held[pl.ds(g, channels, stride=8), :]
            h1 = held[pl.ds(8 * channels + g, channels, stride=8), :]
            d_left = jnp.where(low, h0, pltpu.roll(h1, LANES // 2, 1))
            d_right = jnp.where(low, pltpu.roll(h0, LANES // 2, 1), h1)
            d_proj = jnp.concatenate(
                [
                    (d * factors[n, :, span]).astype(BF16)
                    for n, d in enumerate((d_left, d_left, d_right, d_right))
                ],
                axis=0,
            )
            d_normed = dot(weights, d_proj, ((1,), (0,))) + rest[:, span]
            grad = norm_back(d_normed, units[:, span], invs[:, span], gain_in)
            sums.append(grad + pltpu.roll(grad, LANES // 2, 1))
        turned = jnp.concatenate(sums, axis=0).T
        for k in range(4):
            out[:, (4 * k + b) * LANES : (4 * k + b + 1) * LANES] = turned[k * 16 : (k + 1) * 16]


def shaped(dims, kind):
    return jax.ShapeDtypeStruct(dims, kind)


VMEM = pl.BlockSpec(memory_space=pltpu.VMEM)
SMEM = pl.BlockSpec(memory_space=pltpu.SMEM)


def call(kernel, outs, args, scratch=(), scalars=0, cost=1, limit=16):
    return pl.pallas_call(
        kernel,
        out_shape=outs,
        in_specs=[SMEM] * scalars + [VMEM] * (len(args) - scalars),
        out_specs=jax.tree.map(lambda _: VMEM, outs),
        scratch_shapes=list(scratch),
        compiler_params=pltpu.CompilerParams(vmem_limit_bytes=limit * 2**20),
        cost_estimate=pl.CostEstimate(
            flops=cost * 10**8, bytes_accessed=cost * 10**6, transcendentals=0
        ),
    )(*args)


def solution(mesh):
    rows_n, cols_n, tmpl_n = mesh.shape["row"], mesh.shape["col"], mesh.shape["tmpl"]

    def body(pair, saved, upstream, in_gain, out_gain, w_in, w_out):
        channels = in_gain.shape[0]
        near = channels // rows_n
        quads = cols_n // near
        _, tile_rows, merged = pair.shape
        half = tile_rows // tmpl_n
        in_gain, out_gain = in_gain[None], out_gain[None]
        mine = lax.axis_index("tmpl")
        quad = lax.axis_index("col") // near
        mine1, quad1 = mine[None].astype(jnp.int32), quad[None].astype(jnp.int32)
        cells = tile_rows * merged // channels
        count = cells // LANES

        give = jnp.concatenate(
            [
                lax.dynamic_slice_in_dim(x, (1 - mine) * half, half, 1)
                for x in (pair, saved, upstream)
            ],
            axis=0,
        )
        other = lax.ppermute(give, "tmpl", [(0, 1), (1, 0)])

        send = call(
            spread_kernel,
            shaped((channels, 3 * count, LANES), BF16),
            (pair, saved, upstream, in_gain, out_gain, w_in, w_out),
            scratch=[pltpu.VMEM((channels * 3 * count, LANES), F32)],
            limit=60,
        )
        groups = [
            [r * cols_n + near * q + m for r in range(rows_n) for m in range(near)]
            for q in range(quads)
        ]
        got = lax.all_to_all(send, ("row", "col"), 0, 0, axis_index_groups=groups, tiled=True)
        panel = shaped((LANES, rows_n * tile_rows), BF16)
        d_own, left_all, right_all = call(gather_kernel, (panel,) * 3, (got,))
        far = {}
        for s in (2, 1, 3):
            far[s] = lax.ppermute(
                d_own, "col", [(z, (z - near * s) % cols_n) for z in range(cols_n)]
            )

        factors, rest, units, invs = call(
            prepare_kernel,
            (
                shaped((4, channels, cells), F32),
                shaped((channels, cells), F32),
                shaped((channels, cells), F32),
                shaped((1, cells), F32),
            ),
            (mine1, pair, saved, upstream, other, in_gain, out_gain, w_in, w_out),
            scalars=1,
        )

        back = call(
            product_kernel,
            shaped((tmpl_n * channels, count, LANES), BF16),
            (quad1, left_all, right_all, d_own, far[1], far[2], far[3]),
            scratch=[pltpu.VMEM((LANES, rows_n * tile_rows), F32)] * 2,
            scalars=1,
        )
        groups = [
            [
                (t * rows_n + r) * cols_n + near * q + m
                for t in range(tmpl_n)
                for r in range(rows_n)
                for m in range(near)
            ]
            for q in range(quads)
        ]
        home = lax.all_to_all(
            back, ("tmpl", "row", "col"), 0, 0, axis_index_groups=groups, tiled=True
        )
        return call(
            finish_kernel,
            shaped((half, merged), F32),
            (mine1, home, factors, rest, units, invs, in_gain, w_in),
            scratch=[pltpu.VMEM((tmpl_n * channels * count, LANES), F32)],
            scalars=1,
        )

    in_specs = (P("tmpl", "row", "col"),) * 3 + (P(),) * 4
    out_specs = P(("row", "tmpl"), "col")
    return jax.shard_map(body, mesh=mesh, in_specs=in_specs, out_specs=out_specs, check_vma=False)
```

```python
import jax
import jax.numpy as jnp
from jax import lax
from jax.experimental import pallas as pl
from jax.experimental.pallas import tpu as pltpu
from jax.sharding import PartitionSpec as P


EPSILON = 1e-05
BF16 = jnp.bfloat16
F32 = jnp.float32
LANES = 128


def normalize(values, gain):
    scale = 1.0 / values.shape[0]
    centre = values - jnp.sum(values, axis=0, keepdims=True) * scale
    inv_std = lax.rsqrt(jnp.sum(centre * centre, axis=0, keepdims=True) * scale + EPSILON)
    unit = centre * inv_std
    return unit * gain, unit, inv_std


def norm_back(cotangent, unit, inv_std, gain):
    scale = 1.0 / cotangent.shape[0]
    scaled = cotangent * gain
    centred = scaled - jnp.sum(scaled, axis=0, keepdims=True) * scale
    return (centred - unit * (jnp.sum(scaled * unit, axis=0, keepdims=True) * scale)) * inv_std


def dot(a, b, dims):
    return lax.dot_general(a, b, (dims, ((), ())), preferred_element_type=F32)


def column(gain_ref):
    gain = gain_ref[...]
    return jnp.broadcast_to(gain, (LANES, gain.shape[1])).T[:, :1]


def turn(rows):
    turned = jnp.concatenate(rows, axis=0).astype(F32).T
    half = turned.shape[0] // 2
    return jnp.concatenate([turned[:half], turned[half:]], axis=1)


def swap_groups(values, lane):
    count = len(values)
    values = list(values)
    bit = count // 2
    while bit:
        shift = bit * (LANES // count)
        low = (lane & shift) == 0
        for v in range(count):
            if v & bit == 0:
                a, b = values[v], values[v + bit]
                values[v] = jnp.where(low, a, pltpu.roll(b, shift, 1))
                values[v + bit] = jnp.where(low, pltpu.roll(a, LANES - shift, 1), b)
        bit //= 2
    return values


def lanes_of(rows):
    return lax.broadcasted_iota(jnp.int32, (rows, LANES), 1)


def spread_kernel(*refs):
    given, send, copies, held, arrived = refs[:7], refs[7], refs[8:15], refs[15], refs[16]
    moves = [
        pltpu.make_async_copy(src, dst, arrived.at[n])
        for n, (src, dst) in enumerate(zip(given, copies))
    ]
    for move in moves:
        move.start()
    for n in (3, 4, 5, 6, 0, 1, 2):
        moves[n].wait()
    pair, saved, upstream, in_gain, out_gain, w_in, w_out = copies
    channels = w_out.shape[0]
    gain_in, gain_out = column(in_gain), column(out_gain)
    weights, weights_out = w_in[...], w_out[...]
    for b in range(4):

        def tile(ref):
            return turn([ref[0, :, (4 * k + b) * LANES : (4 * k + b + 1) * LANES] for k in range(4)])

        normed, _, _ = normalize(tile(pair), gain_in)
        proj = dot(weights, normed.astype(BF16), ((0,), (0,)))
        gate = [proj[n * channels : (n + 1) * channels] for n in range(5)]
        left = jax.nn.sigmoid(gate[0]) * gate[1]
        right = jax.nn.sigmoid(gate[2]) * gate[3]
        _, unit, inv = normalize(tile(saved), gain_out)
        d_mixed = (tile(upstream) * jax.nn.sigmoid(gate[4])).astype(BF16)
        d_norm = dot(weights_out, d_mixed, ((1,), (0,)))
        d_prod = norm_back(d_norm, unit, inv, gain_out)
        for n, value in enumerate((d_prod, left, right)):
            for p in range(2):
                at = (n * 8 + 2 * b + p) * channels
                held[at : at + channels, :] = value[:, p * LANES : (p + 1) * LANES]
    for c in range(channels):
        send[c] = held[pl.ds(c, 24, stride=channels), :].astype(BF16)


def collect(got, n, lane):
    for m in range(4):
        for block in range(4):
            parts = swap_groups(
                [
                    got[(4 * block + r) * 4 + m, n * 8 : (n + 1) * 8, :].astype(F32)
                    for r in range(4)
                ],
                lane,
            )
            for k in range(2):
                yield (
                    m * 32 + k * 16,
                    slice(block * LANES, (block + 1) * LANES),
                    jnp.concatenate(parts[2 * k : 2 * k + 2], axis=0).astype(BF16),
                )


def cotangent_kernel(got, out):
    for row, columns, value in collect(got, 0, lanes_of(8)):
        out[row : row + 16, columns] = value


def operand_kernel(mine_ref, got, pair, saved, upstream, left_all, right_all, give):
    lane = lanes_of(8)
    first = pl.multiple_of((1 - mine_ref[0]) * 16, 16)
    for n, ref in enumerate((pair, saved, upstream)):
        give[n] = ref[0, pl.ds(first, 16), :]
    for n, out in ((1, left_all), (2, right_all)):
        for row, columns, value in collect(got, n, lane):
            out[row : row + 16, columns] = value


def product_kernel(quad_ref, left_all, right_all, d0, d1, d2, d3, back, d_left, d_right):
    quad = quad_ref[0]
    total = None
    left = left_all[...]
    for s, d_ref in enumerate((d0, d1, d2, d3)):
        at = pl.multiple_of(lax.rem(quad + s, 4) * LANES, LANES)
        d_s = d_ref[...]
        term = dot(right_all[:, pl.ds(at, LANES)], d_s, ((1,), (0,)))
        total = term if total is None else total + term
        d_right[:, pl.ds(at, LANES)] = dot(left, d_s, ((1,), (1,)))
    d_left[...] = total
    lane = lanes_of(8)
    for m in range(4):
        for block in range(4):
            columns = slice(block * LANES, (block + 1) * LANES)
            chunks = swap_groups(
                [
                    ref[m * 32 + k * 8 : m * 32 + (k + 1) * 8, columns]
                    for ref in (d_left, d_right)
                    for k in range(4)
                ],
                lane,
            )
            for u, chunk in enumerate(chunks):
                r, half = block * 4 + u // 2, u % 2
                back[half * 64 + r * 4 + m] = chunk.astype(BF16)


def prepare_kernel(mine_ref, pair, saved, upstream, other, in_gain, out_gain, w_in, w_out, factors, rest, units, invs):
    channels = w_out.shape[0]
    first = pl.multiple_of(mine_ref[0] * 16, 16)
    gain_in, gain_out = column(in_gain), column(out_gain)
    weights, weights_out = w_in[...], w_out[...]
    for b in range(4):

        def tile(n, ref):
            spans = [slice((4 * k + b) * LANES, (4 * k + b + 1) * LANES) for k in range(4)]
            return turn(
                [ref[0, pl.ds(first, 16), span] for span in spans]
                + [other[n, :, span] for span in spans]
            )

        span = slice(2 * b * LANES, (2 * b + 2) * LANES)
        normed, unit, inv = normalize(tile(0, pair), gain_in)
        units[:, span], invs[:, span] = unit, inv
        proj = dot(weights, normed.astype(BF16), ((0,), (0,)))
        gate = [proj[n * channels : (n + 1) * channels] for n in range(5)]
        for n in range(2):
            sig, linear = jax.nn.sigmoid(gate[2 * n]), gate[2 * n + 1]
            factors[2 * n, :, span] = linear * sig * (1.0 - sig)
            factors[2 * n + 1, :, span] = sig
        normed, _, _ = normalize(tile(1, saved), gain_out)
        mixed = dot(weights_out, normed.astype(BF16), ((0,), (0,)))
        out_gate = jax.nn.sigmoid(gate[4])
        d_og = (tile(2, upstream) * mixed * out_gate * (1.0 - out_gate)).astype(BF16)
        rest[:, span] = dot(weights[:, 4 * channels :], d_og, ((1,), (0,)))


def finish_kernel(mine_ref, home, factors, rest, units, invs, in_gain, w_in, out, held):
    channels = rest.shape[0]
    mine = mine_ref[0]
    gain_in = column(in_gain)
    weights = w_in[:, : 4 * channels]
    for t in range(2):
        base = lax.rem(mine + t, 2) * channels
        for c in range(channels):
            at = (t * channels + c) * 8
            held[at : at + 8, :] = home[base + c].astype(F32)
    low = lanes_of(channels) < LANES // 2
    for b in range(4):
        sums = []
        for p in range(2):
            g = 2 * b + p
            span = slice(g * LANES, (g + 1) * LANES)
            h0 = held[pl.ds(g, channels, stride=8), :]
            h1 = held[pl.ds(8 * channels + g, channels, stride=8), :]
            d_left = jnp.where(low, h0, pltpu.roll(h1, LANES // 2, 1))
            d_right = jnp.where(low, pltpu.roll(h0, LANES // 2, 1), h1)
            d_proj = jnp.concatenate(
                [
                    (d * factors[n, :, span]).astype(BF16)
                    for n, d in enumerate((d_left, d_left, d_right, d_right))
                ],
                axis=0,
            )
            d_normed = dot(weights, d_proj, ((1,), (0,))) + rest[:, span]
            grad = norm_back(d_normed, units[:, span], invs[:, span], gain_in)
            sums.append(grad + pltpu.roll(grad, LANES // 2, 1))
        turned = jnp.concatenate(sums, axis=0).T
        for k in range(4):
            out[:, (4 * k + b) * LANES : (4 * k + b + 1) * LANES] = turned[k * 16 : (k + 1) * 16]


def shaped(dims, kind):
    return jax.ShapeDtypeStruct(dims, kind)


VMEM = pl.BlockSpec(memory_space=pltpu.VMEM)
SMEM = pl.BlockSpec(memory_space=pltpu.SMEM)
HBM = pl.BlockSpec(memory_space=pltpu.HBM)


def call(kernel, outs, args, scratch=(), scalars=0, cost=1, limit=16, space=VMEM):
    return pl.pallas_call(
        kernel,
        out_shape=outs,
        in_specs=[SMEM] * scalars + [space] * (len(args) - scalars),
        out_specs=jax.tree.map(lambda _: VMEM, outs),
        scratch_shapes=list(scratch),
        compiler_params=pltpu.CompilerParams(vmem_limit_bytes=limit * 2**20),
        cost_estimate=pl.CostEstimate(
            flops=cost * 10**8, bytes_accessed=cost * 10**6, transcendentals=0
        ),
    )(*args)


def solution(mesh):
    rows_n, cols_n, tmpl_n = mesh.shape["row"], mesh.shape["col"], mesh.shape["tmpl"]

    def body(pair, saved, upstream, in_gain, out_gain, w_in, w_out):
        channels = in_gain.shape[0]
        near = channels // rows_n
        quads = cols_n // near
        _, tile_rows, merged = pair.shape
        half = tile_rows // tmpl_n
        in_gain, out_gain = in_gain[None], out_gain[None]
        mine = lax.axis_index("tmpl")
        quad = lax.axis_index("col") // near
        mine1, quad1 = mine[None].astype(jnp.int32), quad[None].astype(jnp.int32)
        cells = tile_rows * merged // channels
        count = cells // LANES

        given = (pair, saved, upstream, in_gain, out_gain, w_in, w_out)
        send = call(
            spread_kernel,
            shaped((channels, 3 * count, LANES), BF16),
            given,
            scratch=[pltpu.VMEM(x.shape, x.dtype) for x in given]
            + [
                pltpu.VMEM((channels * 3 * count, LANES), F32),
                pltpu.SemaphoreType.DMA((len(given),)),
            ],
            limit=60,
            space=HBM,
        )
        groups = [
            [r * cols_n + near * q + m for r in range(rows_n) for m in range(near)]
            for q in range(quads)
        ]
        got = lax.all_to_all(send, ("row", "col"), 0, 0, axis_index_groups=groups, tiled=True)
        panel = shaped((LANES, rows_n * tile_rows), BF16)
        d_own = call(cotangent_kernel, panel, (got,))
        left_all, right_all, give = call(
            operand_kernel,
            (panel, panel, shaped((3, half, merged), BF16)),
            (mine1, got, pair, saved, upstream),
            scalars=1,
        )
        other = lax.ppermute(give, "tmpl", [(0, 1), (1, 0)])
        far = {}
        for s in (2, 1, 3):
            far[s] = lax.ppermute(
                d_own, "col", [(z, (z - near * s) % cols_n) for z in range(cols_n)]
            )

        factors, rest, units, invs = call(
            prepare_kernel,
            (
                shaped((4, channels, cells), F32),
                shaped((channels, cells), F32),
                shaped((channels, cells), F32),
                shaped((1, cells), F32),
            ),
            (mine1, pair, saved, upstream, other, in_gain, out_gain, w_in, w_out),
            scalars=1,
        )

        back = call(
            product_kernel,
            shaped((tmpl_n * channels, count, LANES), BF16),
            (quad1, left_all, right_all, d_own, far[1], far[2], far[3]),
            scratch=[pltpu.VMEM((LANES, rows_n * tile_rows), F32)] * 2,
            scalars=1,
        )
        groups = [
            [
                (t * rows_n + r) * cols_n + near * q + m
                for t in range(tmpl_n)
                for r in range(rows_n)
                for m in range(near)
            ]
            for q in range(quads)
        ]
        home = lax.all_to_all(
            back, ("tmpl", "row", "col"), 0, 0, axis_index_groups=groups, tiled=True
        )
        return call(
            finish_kernel,
            shaped((half, merged), F32),
            (mine1, home, factors, rest, units, invs, in_gain, w_in),
            scratch=[pltpu.VMEM((tmpl_n * channels * count, LANES), F32)],
            scalars=1,
        )

    in_specs = (P("tmpl", "row", "col"),) * 3 + (P(),) * 4
    out_specs = P(("row", "tmpl"), "col")
    return jax.shard_map(body, mesh=mesh, in_specs=in_specs, out_specs=out_specs, check_vma=False)
```

```python
import jax
import jax.numpy as jnp
from jax import lax
from jax.experimental import pallas as pl
from jax.experimental.pallas import tpu as pltpu
from jax.sharding import PartitionSpec as P


EPSILON = 1e-05
BF16 = jnp.bfloat16
F32 = jnp.float32
LANES = 128


def normalize(values, gain):
    scale = 1.0 / values.shape[0]
    centre = values - jnp.sum(values, axis=0, keepdims=True) * scale
    inv_std = lax.rsqrt(jnp.sum(centre * centre, axis=0, keepdims=True) * scale + EPSILON)
    unit = centre * inv_std
    return unit * gain, unit, inv_std


def norm_back(cotangent, unit, inv_std, gain):
    scale = 1.0 / cotangent.shape[0]
    scaled = cotangent * gain
    centred = scaled - jnp.sum(scaled, axis=0, keepdims=True) * scale
    return (centred - unit * (jnp.sum(scaled * unit, axis=0, keepdims=True) * scale)) * inv_std


def dot(a, b, dims):
    return lax.dot_general(a, b, (dims, ((), ())), preferred_element_type=F32)


def column(gain_ref):
    gain = gain_ref[...]
    return jnp.broadcast_to(gain, (LANES, gain.shape[1])).T[:, :1]


def turn(rows):
    turned = jnp.concatenate(rows, axis=0).astype(F32).T
    half = turned.shape[0] // 2
    return jnp.concatenate([turned[:half], turned[half:]], axis=1)


def swap_groups(values, lane):
    count = len(values)
    values = list(values)
    bit = count // 2
    while bit:
        shift = bit * (LANES // count)
        low = (lane & shift) == 0
        for v in range(count):
            if v & bit == 0:
                a, b = values[v], values[v + bit]
                values[v] = jnp.where(low, a, pltpu.roll(b, shift, 1))
                values[v + bit] = jnp.where(low, pltpu.roll(a, LANES - shift, 1), b)
        bit //= 2
    return values


def lanes_of(rows):
    return lax.broadcasted_iota(jnp.int32, (rows, LANES), 1)


def spread_kernel(*refs):
    given, send, copies = refs[:7], refs[7], refs[8:15]
    held, staged, arrived, sent = refs[15:]
    moves = [
        pltpu.make_async_copy(src, dst, arrived.at[n])
        for n, (src, dst) in enumerate(zip(given, copies))
    ]
    for move in moves:
        move.start()
    for n in (3, 4, 5, 6, 0, 1, 2):
        moves[n].wait()
    pair, saved, upstream, in_gain, out_gain, w_in, w_out = copies
    channels = w_out.shape[0]
    gain_in, gain_out = column(in_gain), column(out_gain)
    weights, weights_out = w_in[...], w_out[...]

    def tiles(ref):
        return jnp.concatenate(
            [
                turn([ref[0, :, (4 * k + b) * LANES : (4 * k + b + 1) * LANES] for k in range(4)])
                for b in range(4)
            ],
            axis=1,
        )

    def hold(n, first, value):
        for g in range(value.shape[1] // LANES):
            for c in range(channels // 8):
                at = ((c * 3 + n) * 8 + first + g) * 8
                held[at : at + 8, :] = value[8 * c : 8 * c + 8, g * LANES : (g + 1) * LANES]

    normed = normalize(tiles(pair), gain_in)[0].astype(BF16)
    _, unit, inv = normalize(tiles(saved), gain_out)
    up = tiles(upstream)
    mixed = []
    for b in range(4):
        span = slice(2 * b * LANES, (2 * b + 2) * LANES)
        proj = dot(weights, normed[:, span], ((0,), (0,)))
        gate = [proj[n * channels : (n + 1) * channels] for n in range(5)]
        hold(1, 2 * b, jax.nn.sigmoid(gate[0]) * gate[1])
        hold(2, 2 * b, jax.nn.sigmoid(gate[2]) * gate[3])
        mixed.append((up[:, span] * jax.nn.sigmoid(gate[4])).astype(BF16))
    d_norm = dot(weights_out, jnp.concatenate(mixed, axis=1), ((1,), (0,)))
    hold(0, 0, norm_back(d_norm, unit, inv, gain_out))
    leaves = []
    for c in range(channels // 8):
        for u in range(8):
            for n in range(3):
                staged[8 * c + u, 8 * n : 8 * n + 8] = held[
                    pl.ds((c * 3 + n) * 64 + u, 8, stride=8), :
                ].astype(BF16)
        rows = pl.ds(8 * c, 8)
        leaves.append(pltpu.make_async_copy(staged.at[rows], send.at[rows], sent.at[c]))
        leaves[-1].start()
    for leave in leaves:
        leave.wait()


def collect(got, n, lane):
    for m in range(4):
        for block in range(4):
            parts = swap_groups(
                [
                    got[(4 * block + r) * 4 + m, n * 8 : (n + 1) * 8, :].astype(F32)
                    for r in range(4)
                ],
                lane,
            )
            for k in range(2):
                yield (
                    m * 32 + k * 16,
                    slice(block * LANES, (block + 1) * LANES),
                    jnp.concatenate(parts[2 * k : 2 * k + 2], axis=0).astype(BF16),
                )


def cotangent_kernel(got, out):
    for row, columns, value in collect(got, 0, lanes_of(8)):
        out[row : row + 16, columns] = value


def operand_kernel(mine_ref, got, pair, saved, upstream, left_all, right_all, give):
    lane = lanes_of(8)
    first = pl.multiple_of((1 - mine_ref[0]) * 16, 16)
    for n, ref in enumerate((pair, saved, upstream)):
        give[n] = ref[0, pl.ds(first, 16), :]
    for n, out in ((1, left_all), (2, right_all)):
        for row, columns, value in collect(got, n, lane):
            out[row : row + 16, columns] = value


def product_kernel(quad_ref, left_all, right_all, d0, d1, d2, d3, back, d_left, d_right):
    quad = quad_ref[0]
    total = None
    left = left_all[...]
    for s, d_ref in enumerate((d0, d1, d2, d3)):
        at = pl.multiple_of(lax.bitwise_xor(quad, s) * LANES, LANES)
        d_s = d_ref[...]
        term = dot(right_all[:, pl.ds(at, LANES)], d_s, ((1,), (0,)))
        total = term if total is None else total + term
        d_right[:, pl.ds(at, LANES)] = dot(left, d_s, ((1,), (1,)))
    d_left[...] = total
    lane = lanes_of(8)
    for m in range(4):
        for block in range(4):
            columns = slice(block * LANES, (block + 1) * LANES)
            chunks = swap_groups(
                [
                    ref[m * 32 + k * 8 : m * 32 + (k + 1) * 8, columns]
                    for ref in (d_left, d_right)
                    for k in range(4)
                ],
                lane,
            )
            for u, chunk in enumerate(chunks):
                r, half = block * 4 + u // 2, u % 2
                back[half * 64 + r * 4 + m] = chunk.astype(BF16)


def prepare_kernel(mine_ref, pair, saved, upstream, other, in_gain, out_gain, w_in, w_out, factors, rest, units, invs):
    channels = w_out.shape[0]
    first = pl.multiple_of(mine_ref[0] * 16, 16)
    gain_in, gain_out = column(in_gain), column(out_gain)
    weights, weights_out = w_in[...], w_out[...]
    for b in range(4):

        def tile(n, ref):
            spans = [slice((4 * k + b) * LANES, (4 * k + b + 1) * LANES) for k in range(4)]
            return turn(
                [ref[0, pl.ds(first, 16), span] for span in spans]
                + [other[n, :, span] for span in spans]
            )

        span = slice(2 * b * LANES, (2 * b + 2) * LANES)
        normed, unit, inv = normalize(tile(0, pair), gain_in)
        units[:, span], invs[:, span] = unit, inv
        proj = dot(weights, normed.astype(BF16), ((0,), (0,)))
        gate = [proj[n * channels : (n + 1) * channels] for n in range(5)]
        for n in range(2):
            sig, linear = jax.nn.sigmoid(gate[2 * n]), gate[2 * n + 1]
            factors[2 * n, :, span] = linear * sig * (1.0 - sig)
            factors[2 * n + 1, :, span] = sig
        normed, _, _ = normalize(tile(1, saved), gain_out)
        mixed = dot(weights_out, normed.astype(BF16), ((0,), (0,)))
        out_gate = jax.nn.sigmoid(gate[4])
        d_og = (tile(2, upstream) * mixed * out_gate * (1.0 - out_gate)).astype(BF16)
        rest[:, span] = dot(weights[:, 4 * channels :], d_og, ((1,), (0,)))


def finish_kernel(mine_ref, home, factors, rest, units, invs, in_gain, w_in, out, held):
    channels = rest.shape[0]
    mine = mine_ref[0]
    gain_in = column(in_gain)
    weights = w_in[:, : 4 * channels]
    for t in range(2):
        base = lax.rem(mine + t, 2) * channels
        for c in range(channels):
            at = (t * channels + c) * 8
            held[at : at + 8, :] = home[base + c].astype(F32)
    low = lanes_of(channels) < LANES // 2
    d_lefts, d_rights = [], []
    for g in range(8):
        h0 = held[pl.ds(g, channels, stride=8), :]
        h1 = held[pl.ds(8 * channels + g, channels, stride=8), :]
        d_lefts.append(jnp.where(low, h0, pltpu.roll(h1, LANES // 2, 1)))
        d_rights.append(jnp.where(low, pltpu.roll(h0, LANES // 2, 1), h1))
    d_left, d_right = jnp.concatenate(d_lefts, axis=1), jnp.concatenate(d_rights, axis=1)
    d_proj = jnp.concatenate(
        [
            (d * factors[n]).astype(BF16)
            for n, d in enumerate((d_left, d_left, d_right, d_right))
        ],
        axis=0,
    )
    d_normed = dot(weights, d_proj, ((1,), (0,))) + rest[...]
    grad = norm_back(d_normed, units[...], invs[...], gain_in)
    for b in range(4):
        sums = []
        for p in range(2):
            part = grad[:, (2 * b + p) * LANES : (2 * b + p + 1) * LANES]
            sums.append(part + pltpu.roll(part, LANES // 2, 1))
        turned = jnp.concatenate(sums, axis=0).T
        for k in range(4):
            out[:, (4 * k + b) * LANES : (4 * k + b + 1) * LANES] = turned[k * 16 : (k + 1) * 16]


def shaped(dims, kind):
    return jax.ShapeDtypeStruct(dims, kind)


VMEM = pl.BlockSpec(memory_space=pltpu.VMEM)
SMEM = pl.BlockSpec(memory_space=pltpu.SMEM)
HBM = pl.BlockSpec(memory_space=pltpu.HBM)


def call(kernel, outs, args, scratch=(), scalars=0, cost=1, limit=16, space=VMEM, out_space=VMEM):
    return pl.pallas_call(
        kernel,
        out_shape=outs,
        in_specs=[SMEM] * scalars + [space] * (len(args) - scalars),
        out_specs=jax.tree.map(lambda _: out_space, outs),
        scratch_shapes=list(scratch),
        compiler_params=pltpu.CompilerParams(vmem_limit_bytes=limit * 2**20),
        cost_estimate=pl.CostEstimate(
            flops=cost * 10**8, bytes_accessed=cost * 10**6, transcendentals=0
        ),
    )(*args)


def solution(mesh):
    rows_n, cols_n, tmpl_n = mesh.shape["row"], mesh.shape["col"], mesh.shape["tmpl"]

    def body(pair, saved, upstream, in_gain, out_gain, w_in, w_out):
        channels = in_gain.shape[0]
        near = channels // rows_n
        quads = cols_n // near
        _, tile_rows, merged = pair.shape
        half = tile_rows // tmpl_n
        in_gain, out_gain = in_gain[None], out_gain[None]
        mine = lax.axis_index("tmpl")
        quad = lax.axis_index("col") // near
        mine1, quad1 = mine[None].astype(jnp.int32), quad[None].astype(jnp.int32)
        cells = tile_rows * merged // channels
        count = cells // LANES

        given = (pair, saved, upstream, in_gain, out_gain, w_in, w_out)
        send = call(
            spread_kernel,
            shaped((channels, 3 * count, LANES), BF16),
            given,
            scratch=[pltpu.VMEM(x.shape, x.dtype) for x in given]
            + [
                pltpu.VMEM((channels * 3 * count, LANES), F32),
                pltpu.VMEM((channels, 3 * count, LANES), BF16),
                pltpu.SemaphoreType.DMA((len(given),)),
                pltpu.SemaphoreType.DMA((channels // 8,)),
            ],
            limit=60,
            space=HBM,
            out_space=HBM,
        )
        groups = [
            [r * cols_n + near * q + m for r in range(rows_n) for m in range(near)]
            for q in range(quads)
        ]
        got = lax.all_to_all(send, ("row", "col"), 0, 0, axis_index_groups=groups, tiled=True)
        panel = shaped((LANES, rows_n * tile_rows), BF16)
        d_own = call(cotangent_kernel, panel, (got,))
        left_all, right_all, give = call(
            operand_kernel,
            (panel, panel, shaped((3, half, merged), BF16)),
            (mine1, got, pair, saved, upstream),
            scalars=1,
        )
        other = lax.ppermute(give, "tmpl", [(0, 1), (1, 0)])
        far = {}
        for s in (2, 1, 3):
            far[s] = lax.ppermute(
                d_own, "col", [(z, z ^ (near * s)) for z in range(cols_n)]
            )

        factors, rest, units, invs = call(
            prepare_kernel,
            (
                shaped((4, channels, cells), F32),
                shaped((channels, cells), F32),
                shaped((channels, cells), F32),
                shaped((1, cells), F32),
            ),
            (mine1, pair, saved, upstream, other, in_gain, out_gain, w_in, w_out),
            scalars=1,
        )

        back = call(
            product_kernel,
            shaped((tmpl_n * channels, count, LANES), BF16),
            (quad1, left_all, right_all, d_own, far[1], far[2], far[3]),
            scratch=[pltpu.VMEM((LANES, rows_n * tile_rows), F32)] * 2,
            scalars=1,
        )
        groups = [
            [
                (t * rows_n + r) * cols_n + near * q + m
                for t in range(tmpl_n)
                for r in range(rows_n)
                for m in range(near)
            ]
            for q in range(quads)
        ]
        home = lax.all_to_all(
            back, ("tmpl", "row", "col"), 0, 0, axis_index_groups=groups, tiled=True
        )
        return call(
            finish_kernel,
            shaped((half, merged), F32),
            (mine1, home, factors, rest, units, invs, in_gain, w_in),
            scratch=[pltpu.VMEM((tmpl_n * channels * count, LANES), F32)],
            scalars=1,
        )

    in_specs = (P("tmpl", "row", "col"),) * 3 + (P(),) * 4
    out_specs = P(("row", "tmpl"), "col")
    return jax.shard_map(body, mesh=mesh, in_specs=in_specs, out_specs=out_specs, check_vma=False)
```

```python
import functools

import jax
import jax.numpy as jnp
from jax import lax
from jax.experimental import pallas as pl
from jax.experimental.pallas import tpu as pltpu
from jax.sharding import PartitionSpec as P


EPSILON = 1e-05
BF16 = jnp.bfloat16
F32 = jnp.float32
LANES = 128


def normalize(values, gain):
    scale = 1.0 / values.shape[0]
    centre = values - jnp.sum(values, axis=0, keepdims=True) * scale
    inv_std = lax.rsqrt(jnp.sum(centre * centre, axis=0, keepdims=True) * scale + EPSILON)
    unit = centre * inv_std
    return unit * gain, unit, inv_std


def norm_back(cotangent, unit, inv_std, gain):
    scale = 1.0 / cotangent.shape[0]
    scaled = cotangent * gain
    centred = scaled - jnp.sum(scaled, axis=0, keepdims=True) * scale
    return (centred - unit * (jnp.sum(scaled * unit, axis=0, keepdims=True) * scale)) * inv_std


def dot(a, b, dims):
    return lax.dot_general(a, b, (dims, ((), ())), preferred_element_type=F32)


def column(gain_ref):
    gain = gain_ref[...]
    return jnp.broadcast_to(gain, (LANES, gain.shape[1])).T[:, :1]


def turn(rows):
    turned = jnp.concatenate(rows, axis=0).astype(F32).T
    half = turned.shape[0] // 2
    return jnp.concatenate([turned[:half], turned[half:]], axis=1)


def swap_groups(values, lane):
    count = len(values)
    values = list(values)
    bit = count // 2
    while bit:
        shift = bit * (LANES // count)
        low = (lane & shift) == 0
        for v in range(count):
            if v & bit == 0:
                a, b = values[v], values[v + bit]
                values[v] = jnp.where(low, a, pltpu.roll(b, shift, 1))
                values[v + bit] = jnp.where(low, pltpu.roll(a, LANES - shift, 1), b)
        bit //= 2
    return values


def lanes_of(rows):
    return lax.broadcasted_iota(jnp.int32, (rows, LANES), 1)


def spread_kernel(*refs):
    given, send, copies = refs[:7], refs[7], refs[8:15]
    held, staged, arrived, sent = refs[15:]
    moves = [
        pltpu.make_async_copy(src, dst, arrived.at[n])
        for n, (src, dst) in enumerate(zip(given, copies))
    ]
    for move in moves:
        move.start()
    for n in (3, 4, 5, 6, 0, 1, 2):
        moves[n].wait()
    pair, saved, upstream, in_gain, out_gain, w_in, w_out = copies
    channels = w_out.shape[0]
    gain_in, gain_out = column(in_gain), column(out_gain)
    weights, weights_out = w_in[...], w_out[...]

    def tiles(ref):
        return jnp.concatenate(
            [
                turn([ref[0, :, (4 * k + b) * LANES : (4 * k + b + 1) * LANES] for k in range(4)])
                for b in range(4)
            ],
            axis=1,
        )

    def hold(n, first, value):
        for g in range(value.shape[1] // LANES):
            for c in range(channels // 8):
                at = ((c * 3 + n) * 8 + first + g) * 8
                held[at : at + 8, :] = value[8 * c : 8 * c + 8, g * LANES : (g + 1) * LANES]

    normed = normalize(tiles(pair), gain_in)[0].astype(BF16)
    _, unit, inv = normalize(tiles(saved), gain_out)
    up = tiles(upstream)
    mixed = []
    for b in range(4):
        span = slice(2 * b * LANES, (2 * b + 2) * LANES)
        proj = dot(weights, normed[:, span], ((0,), (0,)))
        gate = [proj[n * channels : (n + 1) * channels] for n in range(5)]
        hold(1, 2 * b, jax.nn.sigmoid(gate[0]) * gate[1])
        hold(2, 2 * b, jax.nn.sigmoid(gate[2]) * gate[3])
        mixed.append((up[:, span] * jax.nn.sigmoid(gate[4])).astype(BF16))
    d_norm = dot(weights_out, jnp.concatenate(mixed, axis=1), ((1,), (0,)))
    hold(0, 0, norm_back(d_norm, unit, inv, gain_out))
    leaves = []
    for c in range(channels // 8):
        for u in range(8):
            for n in range(3):
                staged[8 * c + u, 8 * n : 8 * n + 8] = held[
                    pl.ds((c * 3 + n) * 64 + u, 8, stride=8), :
                ].astype(BF16)
        rows = pl.ds(8 * c, 8)
        leaves.append(pltpu.make_async_copy(staged.at[rows], send.at[rows], sent.at[c]))
        leaves[-1].start()
    for leave in leaves:
        leave.wait()


def collect(got, n, lane):
    for m in range(4):
        for block in range(4):
            parts = swap_groups(
                [
                    got[(4 * block + r) * 4 + m, n * 8 : (n + 1) * 8, :].astype(F32)
                    for r in range(4)
                ],
                lane,
            )
            for k in range(2):
                yield (
                    m * 32 + k * 16,
                    slice(block * LANES, (block + 1) * LANES),
                    jnp.concatenate(parts[2 * k : 2 * k + 2], axis=0).astype(BF16),
                )


def cotangent_kernel(got, out):
    for row, columns, value in collect(got, 0, lanes_of(8)):
        out[row : row + 16, columns] = value


def operand_kernel(got, pair, saved, upstream, left_all, right_all, give):
    lane = lanes_of(8)
    first = pl.multiple_of((1 - lax.axis_index("tmpl")) * 16, 16)
    for n, ref in enumerate((pair, saved, upstream)):
        give[n] = ref[0, pl.ds(first, 16), :]
    for n, out in ((1, left_all), (2, right_all)):
        for row, columns, value in collect(got, n, lane):
            out[row : row + 16, columns] = value


def product_kernel(near, left_all, right_all, d0, d1, d2, d3, back, d_left, d_right):
    quad = lax.axis_index("col") // near
    total = None
    left = left_all[...]
    for s, d_ref in enumerate((d0, d1, d2, d3)):
        at = pl.multiple_of(lax.bitwise_xor(quad, s) * LANES, LANES)
        d_s = d_ref[...]
        term = dot(right_all[:, pl.ds(at, LANES)], d_s, ((1,), (0,)))
        total = term if total is None else total + term
        d_right[:, pl.ds(at, LANES)] = dot(left, d_s, ((1,), (1,)))
    d_left[...] = total
    lane = lanes_of(8)
    for m in range(4):
        for block in range(4):
            columns = slice(block * LANES, (block + 1) * LANES)
            chunks = swap_groups(
                [
                    ref[m * 32 + k * 8 : m * 32 + (k + 1) * 8, columns]
                    for ref in (d_left, d_right)
                    for k in range(4)
                ],
                lane,
            )
            for u, chunk in enumerate(chunks):
                r, half = block * 4 + u // 2, u % 2
                back[half * 64 + r * 4 + m] = chunk.astype(BF16)


def prepare_kernel(pair, saved, upstream, other, in_gain, out_gain, w_in, w_out, factors, rest, units, invs):
    channels = w_out.shape[0]
    mine = lax.axis_index("tmpl")
    first = pl.multiple_of(mine * 16, 16)
    gain_in, gain_out = column(in_gain), column(out_gain)
    weights, weights_out = w_in[...], w_out[...]
    for b in range(4):

        def tile(n, ref):
            spans = [slice((4 * k + b) * LANES, (4 * k + b + 1) * LANES) for k in range(4)]
            here = jnp.concatenate([ref[0, pl.ds(first, 16), span] for span in spans], axis=0)
            there = jnp.concatenate([other[n, :, span] for span in spans], axis=0)
            here, there = here.astype(F32), there.astype(F32)
            return turn([jnp.where(mine == 0, here, there), jnp.where(mine == 0, there, here)])

        span = slice(2 * b * LANES, (2 * b + 2) * LANES)
        normed, unit, inv = normalize(tile(0, pair), gain_in)
        units[:, span], invs[:, span] = unit, inv
        proj = dot(weights, normed.astype(BF16), ((0,), (0,)))
        gate = [proj[n * channels : (n + 1) * channels] for n in range(5)]
        for n in range(2):
            sig, linear = jax.nn.sigmoid(gate[2 * n]), gate[2 * n + 1]
            factors[2 * n, :, span] = linear * sig * (1.0 - sig)
            factors[2 * n + 1, :, span] = sig
        normed, _, _ = normalize(tile(1, saved), gain_out)
        mixed = dot(weights_out, normed.astype(BF16), ((0,), (0,)))
        out_gate = jax.nn.sigmoid(gate[4])
        d_og = (tile(2, upstream) * mixed * out_gate * (1.0 - out_gate)).astype(BF16)
        rest[:, span] = dot(weights[:, 4 * channels :], d_og, ((1,), (0,)))


def finish_kernel(home, factors, rest, units, invs, in_gain, w_in, out, held):
    channels = rest.shape[0]
    gain_in = column(in_gain)
    weights = w_in[:, : 4 * channels]
    for t in range(2):
        for c in range(channels):
            at = (t * channels + c) * 8
            held[at : at + 8, :] = home[t * channels + c].astype(F32)
    low = lanes_of(channels) < LANES // 2
    d_lefts, d_rights = [], []
    for g in range(8):
        h0 = held[pl.ds(g, channels, stride=8), :]
        h1 = held[pl.ds(8 * channels + g, channels, stride=8), :]
        d_lefts.append(jnp.where(low, h0, pltpu.roll(h1, LANES // 2, 1)))
        d_rights.append(jnp.where(low, pltpu.roll(h0, LANES // 2, 1), h1))
    d_left, d_right = jnp.concatenate(d_lefts, axis=1), jnp.concatenate(d_rights, axis=1)
    d_proj = jnp.concatenate(
        [
            (d * factors[n]).astype(BF16)
            for n, d in enumerate((d_left, d_left, d_right, d_right))
        ],
        axis=0,
    )
    d_normed = dot(weights, d_proj, ((1,), (0,))) + rest[...]
    grad = norm_back(d_normed, units[...], invs[...], gain_in)
    for b in range(4):
        sums = []
        for p in range(2):
            part = grad[:, (2 * b + p) * LANES : (2 * b + p + 1) * LANES]
            sums.append(part + pltpu.roll(part, LANES // 2, 1))
        turned = jnp.concatenate(sums, axis=0).T
        for k in range(4):
            out[:, (4 * k + b) * LANES : (4 * k + b + 1) * LANES] = turned[k * 16 : (k + 1) * 16]


def shaped(dims, kind):
    return jax.ShapeDtypeStruct(dims, kind)


VMEM = pl.BlockSpec(memory_space=pltpu.VMEM)
HBM = pl.BlockSpec(memory_space=pltpu.HBM)


def call(kernel, outs, args, scratch=(), cost=1, limit=16, space=VMEM, out_space=VMEM):
    return pl.pallas_call(
        kernel,
        out_shape=outs,
        in_specs=[space] * len(args),
        out_specs=jax.tree.map(lambda _: out_space, outs),
        scratch_shapes=list(scratch),
        compiler_params=pltpu.CompilerParams(vmem_limit_bytes=limit * 2**20),
        cost_estimate=pl.CostEstimate(
            flops=cost * 10**8, bytes_accessed=cost * 10**6, transcendentals=0
        ),
    )(*args)


def solution(mesh):
    rows_n, cols_n, tmpl_n = mesh.shape["row"], mesh.shape["col"], mesh.shape["tmpl"]

    def body(pair, saved, upstream, in_gain, out_gain, w_in, w_out):
        channels = in_gain.shape[0]
        near = channels // rows_n
        quads = cols_n // near
        _, tile_rows, merged = pair.shape
        half = tile_rows // tmpl_n
        in_gain, out_gain = in_gain[None], out_gain[None]
        cells = tile_rows * merged // channels
        count = cells // LANES

        given = (pair, saved, upstream, in_gain, out_gain, w_in, w_out)
        send = call(
            spread_kernel,
            shaped((channels, 3 * count, LANES), BF16),
            given,
            scratch=[pltpu.VMEM(x.shape, x.dtype) for x in given]
            + [
                pltpu.VMEM((channels * 3 * count, LANES), F32),
                pltpu.VMEM((channels, 3 * count, LANES), BF16),
                pltpu.SemaphoreType.DMA((len(given),)),
                pltpu.SemaphoreType.DMA((channels // 8,)),
            ],
            limit=60,
            space=HBM,
            out_space=HBM,
        )
        groups = [
            [r * cols_n + near * q + m for r in range(rows_n) for m in range(near)]
            for q in range(quads)
        ]
        got = lax.all_to_all(send, ("row", "col"), 0, 0, axis_index_groups=groups, tiled=True)
        panel = shaped((LANES, rows_n * tile_rows), BF16)
        d_own = call(cotangent_kernel, panel, (got,))
        left_all, right_all, give = call(
        operand_kernel,
        (panel, panel, shaped((3, half, merged), BF16)),
        (got, pair, saved, upstream),
        )
        other = lax.ppermute(give, "tmpl", [(0, 1), (1, 0)])
        far = {}
        for s in (2, 1, 3):
            far[s] = lax.ppermute(
                d_own, "col", [(z, z ^ (near * s)) for z in range(cols_n)]
            )

        factors, rest, units, invs = call(
        prepare_kernel,
        (
            shaped((4, channels, cells), F32),
            shaped((channels, cells), F32),
            shaped((channels, cells), F32),
            shaped((1, cells), F32),
        ),
        (pair, saved, upstream, other, in_gain, out_gain, w_in, w_out),
        )

        back = call(
            functools.partial(product_kernel, near),
            shaped((tmpl_n * channels, count, LANES), BF16),
            (left_all, right_all, d_own, far[1], far[2], far[3]),
            scratch=[pltpu.VMEM((LANES, rows_n * tile_rows), F32)] * 2,
        )
        groups = [
            [
                (t * rows_n + r) * cols_n + near * q + m
                for t in range(tmpl_n)
                for r in range(rows_n)
                for m in range(near)
            ]
            for q in range(quads)
        ]
        home = lax.all_to_all(
            back, ("tmpl", "row", "col"), 0, 0, axis_index_groups=groups, tiled=True
        )
        return call(
            finish_kernel,
            shaped((half, merged), F32),
            (home, factors, rest, units, invs, in_gain, w_in),
            scratch=[pltpu.VMEM((tmpl_n * channels * count, LANES), F32)],
        )

    in_specs = (P("tmpl", "row", "col"),) * 3 + (P(),) * 4
    out_specs = P(("row", "tmpl"), "col")
    return jax.shard_map(body, mesh=mesh, in_specs=in_specs, out_specs=out_specs, check_vma=False)
```

```python
import jax
import jax.numpy as jnp
from jax import lax
from jax.experimental import pallas as pl
from jax.experimental.pallas import tpu as pltpu
from jax.sharding import PartitionSpec as P


EPSILON = 1e-05
BF16 = jnp.bfloat16
F32 = jnp.float32
LANES = 128


def normalize(values, gain):
    scale = 1.0 / values.shape[0]
    centre = values - jnp.sum(values, axis=0, keepdims=True) * scale
    inv_std = lax.rsqrt(jnp.sum(centre * centre, axis=0, keepdims=True) * scale + EPSILON)
    unit = centre * inv_std
    return unit * gain, unit, inv_std


def norm_back(cotangent, unit, inv_std, gain):
    scale = 1.0 / cotangent.shape[0]
    scaled = cotangent * gain
    centred = scaled - jnp.sum(scaled, axis=0, keepdims=True) * scale
    return (centred - unit * (jnp.sum(scaled * unit, axis=0, keepdims=True) * scale)) * inv_std


def dot(a, b, dims):
    return lax.dot_general(a, b, (dims, ((), ())), preferred_element_type=F32)


def column(gain_ref):
    gain = gain_ref[...]
    return jnp.broadcast_to(gain, (LANES, gain.shape[1])).T[:, :1]


def turn(rows):
    turned = jnp.concatenate(rows, axis=0).astype(F32).T
    half = turned.shape[0] // 2
    return jnp.concatenate([turned[:half], turned[half:]], axis=1)


def swap_groups(values, lane):
    count = len(values)
    values = list(values)
    bit = count // 2
    while bit:
        shift = bit * (LANES // count)
        low = (lane & shift) == 0
        for v in range(count):
            if v & bit == 0:
                a, b = values[v], values[v + bit]
                values[v] = jnp.where(low, a, pltpu.roll(b, shift, 1))
                values[v + bit] = jnp.where(low, pltpu.roll(a, LANES - shift, 1), b)
        bit //= 2
    return values


def lanes_of(rows):
    return lax.broadcasted_iota(jnp.int32, (rows, LANES), 1)


def spread_kernel(*refs):
    given, send, copies = refs[:7], refs[7], refs[8:15]
    held, staged, arrived, sent = refs[15:]
    moves = [
        pltpu.make_async_copy(src, dst, arrived.at[n])
        for n, (src, dst) in enumerate(zip(given, copies))
    ]
    for move in moves:
        move.start()
    for n in (3, 4, 5, 6, 0, 1, 2):
        moves[n].wait()
    pair, saved, upstream, in_gain, out_gain, w_in, w_out = copies
    channels = w_out.shape[0]
    gain_in, gain_out = column(in_gain), column(out_gain)
    weights, weights_out = w_in[...], w_out[...]

    def tiles(ref):
        return jnp.concatenate(
            [
                turn([ref[0, :, (4 * k + b) * LANES : (4 * k + b + 1) * LANES] for k in range(4)])
                for b in range(4)
            ],
            axis=1,
        )

    def hold(n, first, value):
        for g in range(value.shape[1] // LANES):
            for c in range(channels // 8):
                at = ((c * 3 + n) * 8 + first + g) * 8
                held[at : at + 8, :] = value[8 * c : 8 * c + 8, g * LANES : (g + 1) * LANES]

    normed = normalize(tiles(pair), gain_in)[0].astype(BF16)
    _, unit, inv = normalize(tiles(saved), gain_out)
    up = tiles(upstream)
    mixed = []
    for b in range(4):
        span = slice(2 * b * LANES, (2 * b + 2) * LANES)
        proj = dot(weights, normed[:, span], ((0,), (0,)))
        gate = [proj[n * channels : (n + 1) * channels] for n in range(5)]
        hold(0, 2 * b, jax.nn.sigmoid(gate[0]) * gate[1])
        hold(1, 2 * b, jax.nn.sigmoid(gate[2]) * gate[3])
        mixed.append((up[:, span] * jax.nn.sigmoid(gate[4])).astype(BF16))
    leaves = []

    def leave_with(part, panels):
        for c in range(channels // 8):
            for u in range(8):
                for n in panels:
                    staged[8 * c + u, 8 * n : 8 * n + 8] = held[
                        pl.ds((c * 3 + n) * 64 + u, 8, stride=8), :
                    ].astype(BF16)
        block = pl.ds(8 * panels[0], 8 * len(panels))
        leaves.append(
            pltpu.make_async_copy(staged.at[:, block], send.at[:, block], sent.at[part])
        )
        leaves[-1].start()

    leave_with(0, (0, 1))
    d_norm = dot(weights_out, jnp.concatenate(mixed, axis=1), ((1,), (0,)))
    hold(2, 0, norm_back(d_norm, unit, inv, gain_out))
    leave_with(1, (2,))
    for leave in leaves:
        leave.wait()


def collect(got, n, lane):
    for m in range(4):
        for block in range(4):
            parts = swap_groups(
                [
                    got[(4 * block + r) * 4 + m, n * 8 : (n + 1) * 8, :].astype(F32)
                    for r in range(4)
                ],
                lane,
            )
            for k in range(2):
                yield (
                    m * 32 + k * 16,
                    slice(block * LANES, (block + 1) * LANES),
                    jnp.concatenate(parts[2 * k : 2 * k + 2], axis=0).astype(BF16),
                )


def cotangent_kernel(got, out):
    for row, columns, value in collect(got, 2, lanes_of(8)):
        out[row : row + 16, columns] = value


def operand_kernel(mine_ref, got, pair, saved, upstream, left_all, right_all, give):
    lane = lanes_of(8)
    first = pl.multiple_of((1 - mine_ref[0]) * 16, 16)
    for n, ref in enumerate((pair, saved, upstream)):
        give[n] = ref[0, pl.ds(first, 16), :]
    for n, out in ((0, left_all), (1, right_all)):
        for row, columns, value in collect(got, n, lane):
            out[row : row + 16, columns] = value


def product_kernel(quad_ref, left_all, right_all, d0, d1, d2, d3, back, d_left, d_right):
    quad = quad_ref[0]
    total = None
    left = left_all[...]
    for s, d_ref in enumerate((d0, d1, d2, d3)):
        at = pl.multiple_of(lax.bitwise_xor(quad, s) * LANES, LANES)
        d_s = d_ref[...]
        term = dot(right_all[:, pl.ds(at, LANES)], d_s, ((1,), (0,)))
        total = term if total is None else total + term
        d_right[:, pl.ds(at, LANES)] = dot(left, d_s, ((1,), (1,)))
    d_left[...] = total
    lane = lanes_of(8)
    for m in range(4):
        for block in range(4):
            columns = slice(block * LANES, (block + 1) * LANES)
            chunks = swap_groups(
                [
                    ref[m * 32 + k * 8 : m * 32 + (k + 1) * 8, columns]
                    for ref in (d_left, d_right)
                    for k in range(4)
                ],
                lane,
            )
            for u, chunk in enumerate(chunks):
                r, half = block * 4 + u // 2, u % 2
                back[half * 64 + r * 4 + m] = chunk.astype(BF16)


def prepare_kernel(mine_ref, pair, saved, upstream, other, in_gain, out_gain, w_in, w_out, factors, rest, units, invs):
    channels = w_out.shape[0]
    first = pl.multiple_of(mine_ref[0] * 16, 16)
    gain_in, gain_out = column(in_gain), column(out_gain)
    weights, weights_out = w_in[...], w_out[...]
    for b in range(4):

        def tile(n, ref):
            spans = [slice((4 * k + b) * LANES, (4 * k + b + 1) * LANES) for k in range(4)]
            return turn(
                [ref[0, pl.ds(first, 16), span] for span in spans]
                + [other[n, :, span] for span in spans]
            )

        span = slice(2 * b * LANES, (2 * b + 2) * LANES)
        normed, unit, inv = normalize(tile(0, pair), gain_in)
        units[:, span], invs[:, span] = unit, inv
        proj = dot(weights, normed.astype(BF16), ((0,), (0,)))
        gate = [proj[n * channels : (n + 1) * channels] for n in range(5)]
        for n in range(2):
            sig, linear = jax.nn.sigmoid(gate[2 * n]), gate[2 * n + 1]
            factors[2 * n, :, span] = linear * sig * (1.0 - sig)
            factors[2 * n + 1, :, span] = sig
        normed, _, _ = normalize(tile(1, saved), gain_out)
        mixed = dot(weights_out, normed.astype(BF16), ((0,), (0,)))
        out_gate = jax.nn.sigmoid(gate[4])
        d_og = (tile(2, upstream) * mixed * out_gate * (1.0 - out_gate)).astype(BF16)
        rest[:, span] = dot(weights[:, 4 * channels :], d_og, ((1,), (0,)))


def finish_kernel(mine_ref, home, factors, rest, units, invs, in_gain, w_in, out, held):
    channels = rest.shape[0]
    mine = mine_ref[0]
    gain_in = column(in_gain)
    weights = w_in[:, : 4 * channels]
    for t in range(2):
        base = lax.rem(mine + t, 2) * channels
        for c in range(channels):
            at = (t * channels + c) * 8
            held[at : at + 8, :] = home[base + c].astype(F32)
    low = lanes_of(channels) < LANES // 2
    d_lefts, d_rights = [], []
    for g in range(8):
        h0 = held[pl.ds(g, channels, stride=8), :]
        h1 = held[pl.ds(8 * channels + g, channels, stride=8), :]
        d_lefts.append(jnp.where(low, h0, pltpu.roll(h1, LANES // 2, 1)))
        d_rights.append(jnp.where(low, pltpu.roll(h0, LANES // 2, 1), h1))
    d_left, d_right = jnp.concatenate(d_lefts, axis=1), jnp.concatenate(d_rights, axis=1)
    d_proj = jnp.concatenate(
        [
            (d * factors[n]).astype(BF16)
            for n, d in enumerate((d_left, d_left, d_right, d_right))
        ],
        axis=0,
    )
    d_normed = dot(weights, d_proj, ((1,), (0,))) + rest[...]
    grad = norm_back(d_normed, units[...], invs[...], gain_in)
    for b in range(4):
        sums = []
        for p in range(2):
            part = grad[:, (2 * b + p) * LANES : (2 * b + p + 1) * LANES]
            sums.append(part + pltpu.roll(part, LANES // 2, 1))
        turned = jnp.concatenate(sums, axis=0).T
        for k in range(4):
            out[:, (4 * k + b) * LANES : (4 * k + b + 1) * LANES] = turned[k * 16 : (k + 1) * 16]


def shaped(dims, kind):
    return jax.ShapeDtypeStruct(dims, kind)


VMEM = pl.BlockSpec(memory_space=pltpu.VMEM)
SMEM = pl.BlockSpec(memory_space=pltpu.SMEM)
HBM = pl.BlockSpec(memory_space=pltpu.HBM)


def call(kernel, outs, args, scratch=(), scalars=0, cost=1, limit=16, space=VMEM, out_space=VMEM):
    return pl.pallas_call(
        kernel,
        out_shape=outs,
        in_specs=[SMEM] * scalars + [space] * (len(args) - scalars),
        out_specs=jax.tree.map(lambda _: out_space, outs),
        scratch_shapes=list(scratch),
        compiler_params=pltpu.CompilerParams(vmem_limit_bytes=limit * 2**20),
        cost_estimate=pl.CostEstimate(
            flops=cost * 10**8, bytes_accessed=cost * 10**6, transcendentals=0
        ),
    )(*args)


def solution(mesh):
    rows_n, cols_n, tmpl_n = mesh.shape["row"], mesh.shape["col"], mesh.shape["tmpl"]

    def body(pair, saved, upstream, in_gain, out_gain, w_in, w_out):
        channels = in_gain.shape[0]
        near = channels // rows_n
        quads = cols_n // near
        _, tile_rows, merged = pair.shape
        half = tile_rows // tmpl_n
        in_gain, out_gain = in_gain[None], out_gain[None]
        mine = lax.axis_index("tmpl")
        quad = lax.axis_index("col") // near
        mine1, quad1 = mine[None].astype(jnp.int32), quad[None].astype(jnp.int32)
        cells = tile_rows * merged // channels
        count = cells // LANES

        given = (pair, saved, upstream, in_gain, out_gain, w_in, w_out)
        send = call(
            spread_kernel,
            shaped((channels, 3 * count, LANES), BF16),
            given,
            scratch=[pltpu.VMEM(x.shape, x.dtype) for x in given]
            + [
                pltpu.VMEM((channels * 3 * count, LANES), F32),
                pltpu.VMEM((channels, 3 * count, LANES), BF16),
                pltpu.SemaphoreType.DMA((len(given),)),
                pltpu.SemaphoreType.DMA((channels // 8,)),
            ],
            limit=60,
            space=HBM,
            out_space=HBM,
        )
        groups = [
            [r * cols_n + near * q + m for r in range(rows_n) for m in range(near)]
            for q in range(quads)
        ]
        got = lax.all_to_all(send, ("row", "col"), 0, 0, axis_index_groups=groups, tiled=True)
        panel = shaped((LANES, rows_n * tile_rows), BF16)
        d_own = call(cotangent_kernel, panel, (got,))
        left_all, right_all, give = call(
            operand_kernel,
            (panel, panel, shaped((3, half, merged), BF16)),
            (mine1, got, pair, saved, upstream),
            scalars=1,
        )
        other = lax.ppermute(give, "tmpl", [(0, 1), (1, 0)])
        far = {}
        for s in (2, 1, 3):
            far[s] = lax.ppermute(
                d_own, "col", [(z, z ^ (near * s)) for z in range(cols_n)]
            )

        factors, rest, units, invs = call(
            prepare_kernel,
            (
                shaped((4, channels, cells), F32),
                shaped((channels, cells), F32),
                shaped((channels, cells), F32),
                shaped((1, cells), F32),
            ),
            (mine1, pair, saved, upstream, other, in_gain, out_gain, w_in, w_out),
            scalars=1,
        )

        back = call(
            product_kernel,
            shaped((tmpl_n * channels, count, LANES), BF16),
            (quad1, left_all, right_all, d_own, far[1], far[2], far[3]),
            scratch=[pltpu.VMEM((LANES, rows_n * tile_rows), F32)] * 2,
            scalars=1,
        )
        groups = [
            [
                (t * rows_n + r) * cols_n + near * q + m
                for t in range(tmpl_n)
                for r in range(rows_n)
                for m in range(near)
            ]
            for q in range(quads)
        ]
        home = lax.all_to_all(
            back, ("tmpl", "row", "col"), 0, 0, axis_index_groups=groups, tiled=True
        )
        return call(
            finish_kernel,
            shaped((half, merged), F32),
            (mine1, home, factors, rest, units, invs, in_gain, w_in),
            scratch=[pltpu.VMEM((tmpl_n * channels * count, LANES), F32)],
            scalars=1,
        )

    in_specs = (P("tmpl", "row", "col"),) * 3 + (P(),) * 4
    out_specs = P(("row", "tmpl"), "col")
    return jax.shard_map(body, mesh=mesh, in_specs=in_specs, out_specs=out_specs, check_vma=False)
```

```python
import jax
import jax.numpy as jnp
from jax import lax
from jax.experimental import pallas as pl
from jax.experimental.pallas import tpu as pltpu
from jax.sharding import PartitionSpec as P


EPSILON = 1e-05
BF16 = jnp.bfloat16
F32 = jnp.float32
LANES = 128


def normalize(values, gain):
    scale = 1.0 / values.shape[0]
    centre = values - jnp.sum(values, axis=0, keepdims=True) * scale
    inv_std = lax.rsqrt(jnp.sum(centre * centre, axis=0, keepdims=True) * scale + EPSILON)
    unit = centre * inv_std
    return unit * gain, unit, inv_std


def norm_back(cotangent, unit, inv_std, gain):
    scale = 1.0 / cotangent.shape[0]
    scaled = cotangent * gain
    centred = scaled - jnp.sum(scaled, axis=0, keepdims=True) * scale
    return (centred - unit * (jnp.sum(scaled * unit, axis=0, keepdims=True) * scale)) * inv_std


def dot(a, b, dims):
    return lax.dot_general(a, b, (dims, ((), ())), preferred_element_type=F32)


def column(gain_ref):
    gain = gain_ref[...]
    return jnp.broadcast_to(gain, (LANES, gain.shape[1])).T[:, :1]


def turn(rows):
    turned = jnp.concatenate(rows, axis=0).astype(F32).T
    half = turned.shape[0] // 2
    return jnp.concatenate([turned[:half], turned[half:]], axis=1)


def swap_groups(values, lane):
    count = len(values)
    values = list(values)
    bit = count // 2
    while bit:
        shift = bit * (LANES // count)
        low = (lane & shift) == 0
        for v in range(count):
            if v & bit == 0:
                a, b = values[v], values[v + bit]
                values[v] = jnp.where(low, a, pltpu.roll(b, shift, 1))
                values[v + bit] = jnp.where(low, pltpu.roll(a, LANES - shift, 1), b)
        bit //= 2
    return values


def lanes_of(rows):
    return lax.broadcasted_iota(jnp.int32, (rows, LANES), 1)


def spread_kernel(*refs):
    given, send, copies = refs[:7], refs[7], refs[8:15]
    held, staged, arrived, sent = refs[15:]
    moves = [
        pltpu.make_async_copy(src, dst, arrived.at[n])
        for n, (src, dst) in enumerate(zip(given, copies))
    ]
    for move in moves:
        move.start()
    for n in (3, 5, 0):
        moves[n].wait()
    pair, saved, upstream, in_gain, out_gain, w_in, w_out = copies
    channels = w_out.shape[0]
    gain_in, weights = column(in_gain), w_in[...]

    def tiles(ref):
        return jnp.concatenate(
            [
                turn([ref[0, :, (4 * k + b) * LANES : (4 * k + b + 1) * LANES] for k in range(4)])
                for b in range(4)
            ],
            axis=1,
        )

    def hold(n, first, value):
        for g in range(value.shape[1] // LANES):
            for c in range(channels // 8):
                at = ((c * 3 + n) * 8 + first + g) * 8
                held[at : at + 8, :] = value[8 * c : 8 * c + 8, g * LANES : (g + 1) * LANES]

    normed = normalize(tiles(pair), gain_in)[0].astype(BF16)
    for n in (4, 6, 1, 2):
        moves[n].wait()
    gain_out, weights_out = column(out_gain), w_out[...]
    _, unit, inv = normalize(tiles(saved), gain_out)
    up = tiles(upstream)
    mixed = []
    for b in range(4):
        span = slice(2 * b * LANES, (2 * b + 2) * LANES)
        proj = dot(weights, normed[:, span], ((0,), (0,)))
        gate = [proj[n * channels : (n + 1) * channels] for n in range(5)]
        hold(0, 2 * b, jax.nn.sigmoid(gate[0]) * gate[1])
        hold(1, 2 * b, jax.nn.sigmoid(gate[2]) * gate[3])
        mixed.append((up[:, span] * jax.nn.sigmoid(gate[4])).astype(BF16))
    leaves = []

    def leave_with(part, panels):
        for c in range(channels // 8):
            for u in range(8):
                for n in panels:
                    staged[8 * c + u, 8 * n : 8 * n + 8] = held[
                        pl.ds((c * 3 + n) * 64 + u, 8, stride=8), :
                    ].astype(BF16)
        block = pl.ds(8 * panels[0], 8 * len(panels))
        leaves.append(
            pltpu.make_async_copy(staged.at[:, block], send.at[:, block], sent.at[part])
        )
        leaves[-1].start()

    leave_with(0, (0, 1))
    d_norm = dot(weights_out, jnp.concatenate(mixed, axis=1), ((1,), (0,)))
    hold(2, 0, norm_back(d_norm, unit, inv, gain_out))
    leave_with(1, (2,))
    for leave in leaves:
        leave.wait()


def collect(got, n, lane):
    for m in range(4):
        for block in range(4):
            parts = swap_groups(
                [
                    got[(4 * block + r) * 4 + m, n * 8 : (n + 1) * 8, :].astype(F32)
                    for r in range(4)
                ],
                lane,
            )
            for k in range(2):
                yield (
                    m * 32 + k * 16,
                    slice(block * LANES, (block + 1) * LANES),
                    jnp.concatenate(parts[2 * k : 2 * k + 2], axis=0).astype(BF16),
                )


def cotangent_kernel(got, out):
    for row, columns, value in collect(got, 2, lanes_of(8)):
        out[row : row + 16, columns] = value


def operand_kernel(mine_ref, got, pair, saved, upstream, left_all, right_all, give):
    lane = lanes_of(8)
    first = pl.multiple_of((1 - mine_ref[0]) * 16, 16)
    for n, ref in enumerate((pair, saved, upstream)):
        give[n] = ref[0, pl.ds(first, 16), :]
    for n, out in ((0, left_all), (1, right_all)):
        for row, columns, value in collect(got, n, lane):
            out[row : row + 16, columns] = value


def product_kernel(quad_ref, left_all, right_all, d0, d1, d2, d3, back, d_left, d_right):
    quad = quad_ref[0]
    total = None
    left = left_all[...]
    for s, d_ref in enumerate((d0, d1, d2, d3)):
        at = pl.multiple_of(lax.bitwise_xor(quad, s) * LANES, LANES)
        d_s = d_ref[...]
        term = dot(right_all[:, pl.ds(at, LANES)], d_s, ((1,), (0,)))
        total = term if total is None else total + term
        d_right[:, pl.ds(at, LANES)] = dot(left, d_s, ((1,), (1,)))
    d_left[...] = total
    lane = lanes_of(8)
    for m in range(4):
        for block in range(4):
            columns = slice(block * LANES, (block + 1) * LANES)
            chunks = swap_groups(
                [
                    ref[m * 32 + k * 8 : m * 32 + (k + 1) * 8, columns]
                    for ref in (d_left, d_right)
                    for k in range(4)
                ],
                lane,
            )
            for u, chunk in enumerate(chunks):
                r, half = block * 4 + u // 2, u % 2
                back[half * 64 + r * 4 + m] = chunk.astype(BF16)


def prepare_kernel(mine_ref, pair, saved, upstream, other, in_gain, out_gain, w_in, w_out, factors, rest, units, invs):
    channels = w_out.shape[0]
    first = pl.multiple_of(mine_ref[0] * 16, 16)
    gain_in, gain_out = column(in_gain), column(out_gain)
    weights, weights_out = w_in[...], w_out[...]
    for b in range(4):

        def tile(n, ref):
            spans = [slice((4 * k + b) * LANES, (4 * k + b + 1) * LANES) for k in range(4)]
            return turn(
                [ref[0, pl.ds(first, 16), span] for span in spans]
                + [other[n, :, span] for span in spans]
            )

        span = slice(2 * b * LANES, (2 * b + 2) * LANES)
        normed, unit, inv = normalize(tile(0, pair), gain_in)
        units[:, span], invs[:, span] = unit, inv
        proj = dot(weights, normed.astype(BF16), ((0,), (0,)))
        gate = [proj[n * channels : (n + 1) * channels] for n in range(5)]
        for n in range(2):
            sig, linear = jax.nn.sigmoid(gate[2 * n]), gate[2 * n + 1]
            factors[2 * n, :, span] = linear * sig * (1.0 - sig)
            factors[2 * n + 1, :, span] = sig
        normed, _, _ = normalize(tile(1, saved), gain_out)
        mixed = dot(weights_out, normed.astype(BF16), ((0,), (0,)))
        out_gate = jax.nn.sigmoid(gate[4])
        d_og = (tile(2, upstream) * mixed * out_gate * (1.0 - out_gate)).astype(BF16)
        rest[:, span] = dot(weights[:, 4 * channels :], d_og, ((1,), (0,)))


def finish_kernel(mine_ref, home, factors, rest, units, invs, in_gain, w_in, out, held):
    channels = rest.shape[0]
    mine = mine_ref[0]
    gain_in = column(in_gain)
    weights = w_in[:, : 4 * channels]
    for t in range(2):
        base = lax.rem(mine + t, 2) * channels
        for c in range(channels):
            at = (t * channels + c) * 8
            held[at : at + 8, :] = home[base + c].astype(F32)
    low = lanes_of(channels) < LANES // 2
    d_lefts, d_rights = [], []
    for g in range(8):
        h0 = held[pl.ds(g, channels, stride=8), :]
        h1 = held[pl.ds(8 * channels + g, channels, stride=8), :]
        d_lefts.append(jnp.where(low, h0, pltpu.roll(h1, LANES // 2, 1)))
        d_rights.append(jnp.where(low, pltpu.roll(h0, LANES // 2, 1), h1))
    d_left, d_right = jnp.concatenate(d_lefts, axis=1), jnp.concatenate(d_rights, axis=1)
    d_proj = jnp.concatenate(
        [
            (d * factors[n]).astype(BF16)
            for n, d in enumerate((d_left, d_left, d_right, d_right))
        ],
        axis=0,
    )
    d_normed = dot(weights, d_proj, ((1,), (0,))) + rest[...]
    grad = norm_back(d_normed, units[...], invs[...], gain_in)
    for b in range(4):
        sums = []
        for p in range(2):
            part = grad[:, (2 * b + p) * LANES : (2 * b + p + 1) * LANES]
            sums.append(part + pltpu.roll(part, LANES // 2, 1))
        turned = jnp.concatenate(sums, axis=0).T
        for k in range(4):
            out[:, (4 * k + b) * LANES : (4 * k + b + 1) * LANES] = turned[k * 16 : (k + 1) * 16]


def shaped(dims, kind):
    return jax.ShapeDtypeStruct(dims, kind)


VMEM = pl.BlockSpec(memory_space=pltpu.VMEM)
SMEM = pl.BlockSpec(memory_space=pltpu.SMEM)
HBM = pl.BlockSpec(memory_space=pltpu.HBM)


def call(kernel, outs, args, scratch=(), scalars=0, cost=1, limit=16, space=VMEM, out_space=VMEM):
    return pl.pallas_call(
        kernel,
        out_shape=outs,
        in_specs=[SMEM] * scalars + [space] * (len(args) - scalars),
        out_specs=jax.tree.map(lambda _: out_space, outs),
        scratch_shapes=list(scratch),
        compiler_params=pltpu.CompilerParams(vmem_limit_bytes=limit * 2**20),
        cost_estimate=pl.CostEstimate(
            flops=cost * 10**8, bytes_accessed=cost * 10**6, transcendentals=0
        ),
    )(*args)


def solution(mesh):
    rows_n, cols_n, tmpl_n = mesh.shape["row"], mesh.shape["col"], mesh.shape["tmpl"]

    def body(pair, saved, upstream, in_gain, out_gain, w_in, w_out):
        channels = in_gain.shape[0]
        near = channels // rows_n
        quads = cols_n // near
        _, tile_rows, merged = pair.shape
        half = tile_rows // tmpl_n
        in_gain, out_gain = in_gain[None], out_gain[None]
        mine = lax.axis_index("tmpl")
        quad = lax.axis_index("col") // near
        mine1, quad1 = mine[None].astype(jnp.int32), quad[None].astype(jnp.int32)
        cells = tile_rows * merged // channels
        count = cells // LANES

        given = (pair, saved, upstream, in_gain, out_gain, w_in, w_out)
        send = call(
            spread_kernel,
            shaped((channels, 3 * count, LANES), BF16),
            given,
            scratch=[pltpu.VMEM(x.shape, x.dtype) for x in given]
            + [
                pltpu.VMEM((channels * 3 * count, LANES), F32),
                pltpu.VMEM((channels, 3 * count, LANES), BF16),
                pltpu.SemaphoreType.DMA((len(given),)),
                pltpu.SemaphoreType.DMA((channels // 8,)),
            ],
            limit=60,
            space=HBM,
            out_space=HBM,
        )
        groups = [
            [r * cols_n + near * q + m for r in range(rows_n) for m in range(near)]
            for q in range(quads)
        ]
        got = lax.all_to_all(send, ("row", "col"), 0, 0, axis_index_groups=groups, tiled=True)
        panel = shaped((LANES, rows_n * tile_rows), BF16)
        d_own = call(cotangent_kernel, panel, (got,))
        left_all, right_all, give = call(
            operand_kernel,
            (panel, panel, shaped((3, half, merged), BF16)),
            (mine1, got, pair, saved, upstream),
            scalars=1,
        )
        other = lax.ppermute(give, "tmpl", [(0, 1), (1, 0)])
        far = {}
        for s in (2, 1, 3):
            far[s] = lax.ppermute(
                d_own, "col", [(z, z ^ (near * s)) for z in range(cols_n)]
            )

        factors, rest, units, invs = call(
            prepare_kernel,
            (
                shaped((4, channels, cells), F32),
                shaped((channels, cells), F32),
                shaped((channels, cells), F32),
                shaped((1, cells), F32),
            ),
            (mine1, pair, saved, upstream, other, in_gain, out_gain, w_in, w_out),
            scalars=1,
        )

        back = call(
            product_kernel,
            shaped((tmpl_n * channels, count, LANES), BF16),
            (quad1, left_all, right_all, d_own, far[1], far[2], far[3]),
            scratch=[pltpu.VMEM((LANES, rows_n * tile_rows), F32)] * 2,
            scalars=1,
        )
        groups = [
            [
                (t * rows_n + r) * cols_n + near * q + m
                for t in range(tmpl_n)
                for r in range(rows_n)
                for m in range(near)
            ]
            for q in range(quads)
        ]
        home = lax.all_to_all(
            back, ("tmpl", "row", "col"), 0, 0, axis_index_groups=groups, tiled=True
        )
        return call(
            finish_kernel,
            shaped((half, merged), F32),
            (mine1, home, factors, rest, units, invs, in_gain, w_in),
            scratch=[pltpu.VMEM((tmpl_n * channels * count, LANES), F32)],
            scalars=1,
        )

    in_specs = (P("tmpl", "row", "col"),) * 3 + (P(),) * 4
    out_specs = P(("row", "tmpl"), "col")
    return jax.shard_map(body, mesh=mesh, in_specs=in_specs, out_specs=out_specs, check_vma=False)
```
